256 devices in a mesh: dp: 8 (over x, core), expert: 32 (over z, y).
Axes of the slice: x: 4, y: 4, z: 8, core: 2. Of those that a mesh axis runs over, the one named last changes fastest.
Arguments:
- tokens: bfloat16 [4096, 2880], P(('dp', 'expert')), may hold values from -200 to 200
- norm_gain: float32 [2880], replicated, may hold values from 0.5 to 4
- router_weight: bfloat16 [2880, 32], replicated, may hold values from -0.02734375 to 0.02734375
- router_bias: float32 [32], replicated, may hold values from -1 to 1
- expert_ids: int32 [4096, 4], P(('dp', 'expert')), may hold values from 0 to 31, all different within a row; in each aligned block of 16 rows (0 to 15, 16 to 31, ...) at most 4 rows name the same one
- placement: int32 [32], replicated, may hold values from 0 to 31, each once
- gate_up: bfloat16 [32, 2, 2880, 2880], P('expert', None, None, 'dp'), may hold values from -0.109375 to 0.109375
- gate_up_bias: float32 [32, 2, 2880], P('expert', None, 'dp'), may hold values from -3 to 3
- down_proj: bfloat16 [32, 2880, 2880], P('expert', 'dp'), may hold values from -0.109375 to 0.109375
- down_bias: float32 [32, 2880], replicated, may hold values from -3 to 3
Outputs:
- mixed: bfloat16 [4096, 2880], P(('dp', 'expert'))
The draws below stay inside these ranges and needn't reach their ends.
Inputs may be any that keep to these rules, and one draw needn't show every extreme that they name: `expert_ids`: in the rows of one device no expert is named more than 4 times; in every draw some device names some expert exactly 4 times. `placement`: every holder index appears once.
All inputs are finite; a program needn't handle non-finite values.
Results may differ from the reference program's by a relative error of at most 0.015.
Values may be sent and summed in bfloat16 or wider, within the bound.
A program may use at most 64 MiB of HBM per device.

```python
import math
import jax
import jax.numpy as jnp
import numpy as np
from jax import lax

D = 2880
FF = 2880
TOPK = 4
TOK_DEV = 16
EXPERTS = 32
CAP = 4
TOKENS = 4096
N_DP = 8
DEVICES = 256


def draw_tokens(key, part):
    key_rows = jax.random.fold_in(key, 11)
    key_cols = jax.random.fold_in(key, 12)
    key_vals = jax.random.fold_in(key, 13)
    row_scale = jnp.exp(jax.random.uniform(key_rows, (TOKENS, 1), jnp.float32, -2.3, 2.3))
    col_scale = jnp.exp(jax.random.uniform(key_cols, (1, D), jnp.float32, -1.15, 1.15))
    values = jnp.clip(jax.random.normal(key_vals, (TOKENS, D), jnp.float32), -5.0, 5.0)
    return (values * row_scale * col_scale).astype(jnp.bfloat16)


def block_levels(own_key, extent, split, low, largest):
    def one(dim, parts):
        heights = jax.random.uniform(jax.random.fold_in(jax.random.fold_in(own_key, 6), dim), (parts,), jnp.float32, low / len(split), largest / len(split))
        return jnp.repeat(jnp.exp(heights), extent[dim] // parts).reshape((-1,) + (1,) * (len(extent) - dim - 1))

    factor_of = one(*split[0])
    for cut in split[1:]:
        factor_of = factor_of * one(*cut)
    return factor_of


def routed_block(key, own, number, rows, count, top, bound, slope):
    order = jax.random.permutation(key, count)
    heavy_load, usual = portions_of(count, rows * top, bound, slope, True), portions_of(count, rows * top, bound, slope, False)
    places = jnp.arange(count)

    def named(lengths, rotation):
        used = int((lengths > 0).sum())
        fixed = max(1, used // 4)
        moved = fixed + (places - fixed + rotation * (used - fixed)) % max(1, count - fixed)
        return jnp.zeros((count,), jnp.int32).at[order[jnp.where(places < fixed, places, moved)]].set(jnp.asarray(lengths, jnp.int32))

    lengths = jnp.where(number % 4 == 0, named(heavy_load, number // 4), named(usual, number - number // 4 - 1))
    mixed = jax.random.permutation(jax.random.fold_in(own, 3), count)
    source_of, receiver = mixed[0:count // 2 * 2:2], mixed[1:count // 2 * 2:2]
    margin = jnp.minimum(lengths[source_of] - 1, bound - lengths[receiver]) // 2
    margin = jnp.where((source_of == order[0]) | (receiver == order[0]) | (lengths[receiver] == 0), 0, jnp.maximum(margin, 0))
    moved = jax.random.randint(jax.random.fold_in(own, 4), (count // 2,), 0, 1 << 20) % (margin + 1)
    lengths = lengths.at[source_of].add(-moved).at[receiver].add(moved)
    members = jnp.searchsorted(jnp.cumsum(lengths), jnp.arange(rows * top), side="right").astype(jnp.int32)
    grid = members.reshape(top, rows).T
    grid = grid[jax.random.permutation(jax.random.fold_in(own, 1), rows)]
    rotation = jax.random.randint(jax.random.fold_in(own, 2), (rows, 1), 0, top)
    return jnp.take_along_axis(grid, (jnp.arange(top)[None, :] + rotation) % top, axis=1)


def portions_of(count, total, bound, lean, full):
    weights = [(1 << 20) // math.isqrt(standing ** lean) + 1 for standing in range(1, count + 1)]
    largest = bound if full else min(bound, max(-(-total // count), total * weights[0] // sum(weights)))
    least = 1 if total - largest >= count - 1 else 0
    given, surplus = [largest] + [least] * (count - 1), total - largest - least * (count - 1)
    while surplus > 0:
        free = [i for i in range(1, count) if given[i] < largest] or [i for i in range(1, count) if given[i] < bound]
        mass, left = sum([weights[i] for i in free]), surplus
        for i in free:
            more = min(bound - given[i], max(1, left * weights[i] // mass), surplus)
            given[i] = given[i] + more
            surplus = surplus - more
    return np.array(given)


def scatter_about(stream_key, dims, scale, bound, pieces=(), held_as=jnp.bfloat16):
    result = jax.random.normal(stream_key, dims, jnp.float32) * scale
    if len(pieces) > 0:
        result = block_levels(stream_key, dims, pieces, -0.22, 0.18) * result
    return jnp.clip(result, min=-bound, max=bound).astype(held_as)


def setup_inputs(seed: int = 0) -> dict:
    arg_keys = jax.random.split(jax.random.key(seed), 11)
    tokens = draw_tokens(jax.random.fold_in(arg_keys[10], 71), 0)
    norm_gain = jnp.clip(jnp.exp(jax.random.uniform(arg_keys[1], (D,), jnp.float32, math.log(0.5), math.log(4.0))), 0.5, 4.0)
    router_weight = scatter_about(arg_keys[2], (D, EXPERTS), (16 * D) ** -0.5, 0.02734375)
    router_bias = scatter_about(arg_keys[3], (EXPERTS,), 0.3, 1.0, (), jnp.float32)
    expert_ids_keys = jax.random.split(jax.random.fold_in(arg_keys[4], 1), TOKENS // TOK_DEV)
    expert_ids_turns = jax.random.permutation(jax.random.fold_in(arg_keys[4], 3), TOKENS // TOK_DEV)
    expert_ids = jax.vmap(lambda own, number: routed_block(jax.random.fold_in(arg_keys[4], 2), own, number, TOK_DEV, EXPERTS, TOPK, CAP, 1))(expert_ids_keys, expert_ids_turns).reshape((TOKENS, TOPK))
    placement = jax.random.permutation(arg_keys[5], EXPERTS).astype(jnp.int32)
    gate_up = scatter_about(arg_keys[6], (EXPERTS, 2, D, FF), D ** -0.5, 0.109375, ((0, 32), (3, 8)))
    gate_up_bias = scatter_about(arg_keys[7], (EXPERTS, 2, FF), 0.5, 3.0, ((0, 32), (2, 8)), jnp.float32)
    down_proj = scatter_about(arg_keys[8], (EXPERTS, FF, D), FF ** -0.5, 0.109375, ((0, 32), (1, 8)))
    down_bias = scatter_about(arg_keys[9], (EXPERTS, D), 0.5, 3.0, (), jnp.float32)
    return {"tokens": tokens, "norm_gain": norm_gain, "router_weight": router_weight, "router_bias": router_bias, "expert_ids": expert_ids, "placement": placement, "gate_up": gate_up, "gate_up_bias": gate_up_bias, "down_proj": down_proj, "down_bias": down_bias}


EPS = 1e-05
LIMIT = 7.0
ALPHA = 1.702

def normalize(tokens, norm_gain):
    values = tokens.astype(jnp.float32)
    mean_square = lax.optimization_barrier(jnp.mean(values * values, axis=-1, keepdims=True))
    return (values * lax.rsqrt(mean_square + EPS) * norm_gain).astype(jnp.bfloat16)

def routing(normed, router_weight, router_bias, expert_ids):
    logits = jnp.dot(normed, router_weight, preferred_element_type=jnp.float32) + router_bias
    expert_range = jnp.arange(logits.shape[1], dtype=jnp.int32)
    matches = expert_ids[:, :, None] == expert_range[None, None, :]
    picked = lax.optimization_barrier(jnp.sum(jnp.where(matches, logits[:, None, :], 0.0), axis=2))
    powers = jnp.exp(picked)
    return powers / lax.optimization_barrier(jnp.sum(powers, axis=1, keepdims=True))

def lookup(expert_ids, placement):
    expert_range = jnp.arange(placement.shape[0], dtype=jnp.int32)
    matches = expert_ids[:, :, None] == expert_range[None, None, :]
    return lax.optimization_barrier(jnp.sum(jnp.where(matches, placement[None, None, :], 0), axis=2)).astype(jnp.int32)

def slot_positions(columns, experts):
    flat_ids = columns.reshape(-1)
    expert_range = jnp.arange(experts, dtype=jnp.int32)
    onehot = (flat_ids[:, None] == expert_range[None, :]).astype(jnp.int32)
    before = (jnp.cumsum(onehot, axis=0) - onehot).astype(jnp.int32)
    return lax.optimization_barrier(jnp.sum(before * onehot, axis=1)).astype(jnp.int32).reshape(columns.shape)

def swiglu(gate_value, up_value):
    gate_value = jnp.minimum(gate_value, LIMIT)
    up_value = jnp.clip(up_value, -LIMIT, LIMIT)
    return (up_value + 1.0) * gate_value * jax.nn.sigmoid(ALPHA * gate_value)

def reference(tokens, norm_gain, router_weight, router_bias, expert_ids, placement, gate_up, gate_up_bias, down_proj, down_bias):
    normed = normalize(tokens, norm_gain)
    weights = routing(normed, router_weight, router_bias, expert_ids)
    columns = lookup(expert_ids, placement)
    slot_index = jax.vmap(lambda grouped: slot_positions(grouped, EXPERTS))(columns.reshape(DEVICES, TOK_DEV, TOPK)).reshape(TOKENS, TOPK)
    token_index = jnp.broadcast_to(jnp.arange(TOKENS, dtype=jnp.int32)[:, None], (TOKENS, TOPK)).astype(jnp.int32)
    position = (token_index // TOK_DEV * CAP + slot_index).astype(jnp.int32)
    rows_of = jnp.zeros((EXPERTS, DEVICES * CAP), jnp.int32)
    rows_of = rows_of.at[columns.reshape(-1), position.reshape(-1)].set(token_index.reshape(-1))
    group_width = FF // N_DP

    def expert_rows(column):
        row_block = normed[rows_of[column]].astype(jnp.float32)
        stacked = gate_up[column].astype(jnp.float32)
        gate_value = jnp.dot(row_block, stacked[0], precision=lax.Precision.HIGHEST) + gate_up_bias[column, 0]
        up_value = jnp.dot(row_block, stacked[1], precision=lax.Precision.HIGHEST) + gate_up_bias[column, 1]
        hidden = lax.optimization_barrier(swiglu(gate_value, up_value).astype(jnp.bfloat16)).astype(jnp.float32)
        hidden_split = hidden.reshape(hidden.shape[0], N_DP, group_width)
        down_split = down_proj[column].astype(jnp.float32).reshape(N_DP, group_width, D)
        partials = jnp.einsum('rdf,dfo->dro', hidden_split, down_split, precision=lax.Precision.HIGHEST)
        partials = lax.optimization_barrier(partials.astype(jnp.bfloat16)).astype(jnp.float32)
        summed = lax.optimization_barrier(jnp.sum(partials, axis=0)) + down_bias[column]
        return summed.astype(jnp.bfloat16)
    outputs = lax.map(expert_rows, jnp.arange(EXPERTS, dtype=jnp.int32))
    picked = outputs[columns, position].astype(jnp.float32)
    return lax.optimization_barrier(jnp.sum(weights[:, :, None] * picked, axis=1)).astype(jnp.bfloat16)
```

```python
import jax
import jax.numpy as jnp
from jax import lax
from jax.sharding import PartitionSpec as P

TOPK = 4


EPS = 1e-05
LIMIT = 7.0
ALPHA = 1.702


def normalize(tokens, norm_gain):
    values = tokens.astype(jnp.float32)
    mean_square = jnp.mean(values * values, axis=-1, keepdims=True)
    return (values * lax.rsqrt(mean_square + EPS) * norm_gain).astype(jnp.bfloat16)


def routing(normed, router_weight, router_bias, expert_ids):
    logits = jnp.dot(normed, router_weight, preferred_element_type=jnp.float32) + router_bias
    expert_range = jnp.arange(logits.shape[1], dtype=jnp.int32)
    matches = expert_ids[:, :, None] == expert_range[None, None, :]
    picked = jnp.sum(jnp.where(matches, logits[:, None, :], 0.0), axis=2)
    powers = jnp.exp(picked)
    return powers / jnp.sum(powers, axis=1, keepdims=True)


def lookup(expert_ids, placement):
    expert_range = jnp.arange(placement.shape[0], dtype=jnp.int32)
    matches = expert_ids[:, :, None] == expert_range[None, None, :]
    return jnp.sum(jnp.where(matches, placement[None, None, :], 0), axis=2)


def slot_positions(columns, experts):
    flat_ids = columns.reshape(-1)
    expert_range = jnp.arange(experts, dtype=jnp.int32)
    onehot = (flat_ids[:, None] == expert_range[None, :]).astype(jnp.int32)
    before = jnp.cumsum(onehot, axis=0) - onehot
    return jnp.sum(before * onehot, axis=1).reshape(columns.shape)


def swiglu(gate_value, up_value):
    gate_value = jnp.minimum(gate_value, LIMIT)
    up_value = jnp.clip(up_value, -LIMIT, LIMIT)
    return (up_value + 1.0) * gate_value * jax.nn.sigmoid(ALPHA * gate_value)


def body(
    tokens,
    norm_gain,
    router_weight,
    router_bias,
    expert_ids,
    placement,
    gate_up,
    gate_up_bias,
    down_proj,
    down_bias,
):
    tok_dev = tokens.shape[0]
    model_width = tokens.shape[1]
    experts = placement.shape[0]
    capacity = max(2, 2 * tok_dev * TOPK // experts)
    dp_count = lax.axis_size("dp")
    expert_count = lax.axis_size("expert")
    normed = normalize(tokens, norm_gain)
    weights = routing(normed, router_weight, router_bias, expert_ids)
    columns = lookup(expert_ids, placement)
    target_row = columns * capacity + slot_positions(columns, experts)
    targets = jnp.arange(experts * capacity, dtype=jnp.int32)
    dispatch = jnp.sum(
        (target_row[:, :, None] == targets[None, None, :]).astype(jnp.int32), axis=1
    ).astype(jnp.bfloat16)
    outgoing = jnp.dot(dispatch.T, normed, preferred_element_type=jnp.float32).astype(jnp.bfloat16)
    outgoing = outgoing.reshape(experts, capacity, model_width)
    gate_weight = gate_up[0, 0]
    up_weight = gate_up[0, 1]
    gate_bias = gate_up_bias[0, 0]
    up_bias = gate_up_bias[0, 1]
    down_weight = down_proj[0]
    group_width = gate_weight.shape[1]
    row_block = lax.all_to_all(outgoing, "expert", split_axis=0, concat_axis=0, tiled=True)
    row_block = lax.all_gather(row_block, "dp", axis=0, tiled=False)
    flat_rows = row_block.reshape(-1, model_width)
    gate_value = jnp.dot(flat_rows, gate_weight, preferred_element_type=jnp.float32) + gate_bias
    up_value = jnp.dot(flat_rows, up_weight, preferred_element_type=jnp.float32) + up_bias
    hidden = swiglu(gate_value, up_value).astype(jnp.bfloat16)
    hidden = hidden.reshape(row_block.shape[:-1] + (group_width,))

    def down_block(row_block):
        return jnp.dot(row_block, down_weight, preferred_element_type=jnp.float32).astype(
            jnp.bfloat16
        )

    partials = lax.map(down_block, hidden.reshape(dp_count, -1, group_width))
    partials = partials.reshape(dp_count, expert_count, capacity, model_width)
    reduced_parts = lax.psum_scatter(partials, "dp", scatter_dimension=0, tiled=True)
    reduced_parts = reduced_parts.reshape(expert_count, capacity, model_width)
    reduced = lax.all_to_all(reduced_parts, "expert", split_axis=0, concat_axis=0, tiled=True)
    reduced = reduced.astype(jnp.float32)
    reduced = reduced.reshape(experts, capacity, model_width) + down_bias[:, None, :]
    returned = reduced.astype(jnp.bfloat16).reshape(experts * capacity, model_width)
    picked = (
        returned[target_row.reshape(-1)].reshape(tok_dev, TOPK, model_width).astype(jnp.float32)
    )
    return jnp.sum(weights[:, :, None] * picked, axis=1).astype(jnp.bfloat16)


def solution(mesh):
    return jax.shard_map(
        body,
        mesh=mesh,
        in_specs=(
            P(("dp", "expert"), None),
            P(),
            P(),
            P(),
            P(("dp", "expert"), None),
            P(),
            P("expert", None, None, "dp"),
            P("expert", None, "dp"),
            P("expert", "dp", None),
            P(),
        ),
        out_specs=P(("dp", "expert"), None),
        check_vma=False,
    )
```

```python
import jax
import jax.numpy as jnp
from jax import lax
from jax.sharding import Mesh, PartitionSpec as P

TOPK = 4


EPS = 1e-05
LIMIT = 7.0
ALPHA = 1.702


def normalize(tokens, norm_gain):
    values = tokens.astype(jnp.float32)
    mean_square = jnp.mean(values * values, axis=-1, keepdims=True)
    return (values * lax.rsqrt(mean_square + EPS) * norm_gain).astype(jnp.bfloat16)


def routing(normed, router_weight, router_bias, expert_ids):
    logits = jnp.dot(normed, router_weight, preferred_element_type=jnp.float32) + router_bias
    expert_range = jnp.arange(logits.shape[1], dtype=jnp.int32)
    matches = expert_ids[:, :, None] == expert_range[None, None, :]
    picked = jnp.sum(jnp.where(matches, logits[:, None, :], 0.0), axis=2)
    powers = jnp.exp(picked)
    return powers / jnp.sum(powers, axis=1, keepdims=True)


def lookup(expert_ids, placement):
    expert_range = jnp.arange(placement.shape[0], dtype=jnp.int32)
    matches = expert_ids[:, :, None] == expert_range[None, None, :]
    return jnp.sum(jnp.where(matches, placement[None, None, :], 0), axis=2)


def slot_positions(columns, experts):
    flat_ids = columns.reshape(-1)
    expert_range = jnp.arange(experts, dtype=jnp.int32)
    onehot = (flat_ids[:, None] == expert_range[None, :]).astype(jnp.int32)
    before = jnp.cumsum(onehot, axis=0) - onehot
    return jnp.sum(before * onehot, axis=1).reshape(columns.shape)


def swiglu(gate_value, up_value):
    gate_value = jnp.minimum(gate_value, LIMIT)
    up_value = jnp.clip(up_value, -LIMIT, LIMIT)
    return (up_value + 1.0) * gate_value * jax.nn.sigmoid(ALPHA * gate_value)


def body(
    tokens,
    norm_gain,
    router_weight,
    router_bias,
    expert_ids,
    placement,
    gate_up,
    gate_up_bias,
    down_proj,
    down_bias,
):
    tok_dev = tokens.shape[0]
    model_width = tokens.shape[1]
    experts = placement.shape[0]
    capacity = max(2, 2 * tok_dev * TOPK // experts)
    expert_count = lax.axis_size("expert")
    normed = normalize(tokens, norm_gain)
    weights = routing(normed, router_weight, router_bias, expert_ids)
    columns = lookup(expert_ids, placement)
    target_row = columns * capacity + slot_positions(columns, experts)
    targets = jnp.arange(experts * capacity, dtype=jnp.int32)
    dispatch = jnp.sum(
        (target_row[:, :, None] == targets[None, None, :]).astype(jnp.int32), axis=1
    ).astype(jnp.bfloat16)
    outgoing = jnp.dot(dispatch.T, normed, preferred_element_type=jnp.float32).astype(jnp.bfloat16)
    outgoing = outgoing.reshape(experts, capacity, model_width)
    gate_weight = gate_up[0, 0]
    up_weight = gate_up[0, 1]
    gate_bias = gate_up_bias[0, 0]
    up_bias = gate_up_bias[0, 1]
    down_weight = down_proj[0]
    group_width = gate_weight.shape[1]
    row_block = lax.all_to_all(outgoing, "expert", split_axis=0, concat_axis=0, tiled=True)
    row_block = row_block.reshape(experts * capacity, model_width)
    row_block = lax.all_gather(row_block, "dpx", axis=0, tiled=True)
    flat_rows = lax.all_gather(row_block, "dpc", axis=0, tiled=True)
    gate_value = jnp.dot(flat_rows, gate_weight, preferred_element_type=jnp.float32) + gate_bias
    up_value = jnp.dot(flat_rows, up_weight, preferred_element_type=jnp.float32) + up_bias
    hidden = swiglu(gate_value, up_value).astype(jnp.bfloat16)
    partials = jnp.dot(hidden, down_weight, preferred_element_type=jnp.float32).astype(jnp.bfloat16)
    reduced_parts = lax.psum_scatter(partials, "dpc", scatter_dimension=0, tiled=True)
    reduced_parts = lax.psum_scatter(reduced_parts, "dpx", scatter_dimension=0, tiled=True)
    reduced_parts = reduced_parts.reshape(expert_count, capacity, model_width)
    reduced = lax.all_to_all(reduced_parts, "expert", split_axis=0, concat_axis=0, tiled=True)
    reduced = reduced.astype(jnp.float32)
    reduced = reduced.reshape(experts, capacity, model_width) + down_bias[:, None, :]
    returned = reduced.astype(jnp.bfloat16).reshape(experts * capacity, model_width)
    picked = (
        returned[target_row.reshape(-1)].reshape(tok_dev, TOPK, model_width).astype(jnp.float32)
    )
    return jnp.sum(weights[:, :, None] * picked, axis=1).astype(jnp.bfloat16)


def solution(mesh):
    dp_size = mesh.shape["dp"]
    cores = 2 if dp_size % 2 == 0 else 1
    split_mesh = Mesh(
        mesh.devices.reshape(dp_size // cores, cores, mesh.shape["expert"]),
        ("dpx", "dpc", "expert"),
    )
    dp = ("dpx", "dpc")
    return jax.shard_map(
        body,
        mesh=split_mesh,
        in_specs=(
            P(("dpx", "dpc", "expert"), None),
            P(),
            P(),
            P(),
            P(("dpx", "dpc", "expert"), None),
            P(),
            P("expert", None, None, dp),
            P("expert", None, dp),
            P("expert", dp, None),
            P(),
        ),
        out_specs=P(("dpx", "dpc", "expert"), None),
        check_vma=False,
    )
```

```python
import jax
import jax.numpy as jnp
from jax import lax
from jax.sharding import PartitionSpec as P

TOPK = 4


EPS = 1e-05
LIMIT = 7.0
ALPHA = 1.702


def normalize(tokens, norm_gain):
    values = tokens.astype(jnp.float32)
    mean_square = jnp.mean(values * values, axis=-1, keepdims=True)
    return (values * lax.rsqrt(mean_square + EPS) * norm_gain).astype(jnp.bfloat16)


def routing(normed, router_weight, router_bias, expert_ids):
    logits = jnp.dot(normed, router_weight, preferred_element_type=jnp.float32) + router_bias
    expert_range = jnp.arange(logits.shape[1], dtype=jnp.int32)
    matches = expert_ids[:, :, None] == expert_range[None, None, :]
    picked = jnp.sum(jnp.where(matches, logits[:, None, :], 0.0), axis=2)
    powers = jnp.exp(picked)
    return powers / jnp.sum(powers, axis=1, keepdims=True)


def lookup(expert_ids, placement):
    expert_range = jnp.arange(placement.shape[0], dtype=jnp.int32)
    matches = expert_ids[:, :, None] == expert_range[None, None, :]
    return jnp.sum(jnp.where(matches, placement[None, None, :], 0), axis=2)


def slot_positions(columns, experts):
    flat_ids = columns.reshape(-1)
    expert_range = jnp.arange(experts, dtype=jnp.int32)
    onehot = (flat_ids[:, None] == expert_range[None, :]).astype(jnp.int32)
    before = jnp.cumsum(onehot, axis=0) - onehot
    return jnp.sum(before * onehot, axis=1).reshape(columns.shape)


def swiglu(gate_value, up_value):
    gate_value = jnp.minimum(gate_value, LIMIT)
    up_value = jnp.clip(up_value, -LIMIT, LIMIT)
    return (up_value + 1.0) * gate_value * jax.nn.sigmoid(ALPHA * gate_value)


def body(
    tokens,
    norm_gain,
    router_weight,
    router_bias,
    expert_ids,
    placement,
    gate_up,
    gate_up_bias,
    down_proj,
    down_bias,
):
    tok_dev = tokens.shape[0]
    model_width = tokens.shape[1]
    experts = placement.shape[0]
    capacity = max(2, 2 * tok_dev * TOPK // experts)
    expert_count = lax.axis_size("expert")
    normed = normalize(tokens, norm_gain)
    weights = routing(normed, router_weight, router_bias, expert_ids)
    columns = lookup(expert_ids, placement)
    target_row = columns * capacity + slot_positions(columns, experts)
    targets = jnp.arange(experts * capacity, dtype=jnp.int32)
    dispatch = jnp.sum(
        (target_row[:, :, None] == targets[None, None, :]).astype(jnp.int32), axis=1
    ).astype(jnp.bfloat16)
    outgoing = jnp.dot(dispatch.T, normed, preferred_element_type=jnp.float32).astype(jnp.bfloat16)
    outgoing = outgoing.reshape(experts, capacity, model_width)
    gate_weight = gate_up[0, 0]
    up_weight = gate_up[0, 1]
    gate_bias = gate_up_bias[0, 0]
    up_bias = gate_up_bias[0, 1]
    down_weight = down_proj[0]
    group_width = gate_weight.shape[1]
    row_block = lax.all_to_all(outgoing, "expert", split_axis=0, concat_axis=0, tiled=True)
    row_block = row_block.reshape(experts * capacity, model_width)
    flat_rows = lax.all_gather(row_block, "dp", axis=0, tiled=True)
    gate_value = jnp.dot(flat_rows, gate_weight, preferred_element_type=jnp.float32) + gate_bias
    up_value = jnp.dot(flat_rows, up_weight, preferred_element_type=jnp.float32) + up_bias
    hidden = swiglu(gate_value, up_value).astype(jnp.bfloat16)
    partials = jnp.dot(hidden, down_weight, preferred_element_type=jnp.float32).astype(jnp.bfloat16)
    reduced_parts = lax.psum_scatter(partials, "dp", scatter_dimension=0, tiled=True)
    reduced_parts = reduced_parts.reshape(expert_count, capacity, model_width)
    reduced = lax.all_to_all(reduced_parts, "expert", split_axis=0, concat_axis=0, tiled=True)
    reduced = reduced.astype(jnp.float32)
    reduced = reduced.reshape(experts, capacity, model_width) + down_bias[:, None, :]
    returned = reduced.astype(jnp.bfloat16).reshape(experts * capacity, model_width)
    picked = (
        returned[target_row.reshape(-1)].reshape(tok_dev, TOPK, model_width).astype(jnp.float32)
    )
    return jnp.sum(weights[:, :, None] * picked, axis=1).astype(jnp.bfloat16)


def solution(mesh):
    return jax.shard_map(
        body,
        mesh=mesh,
        in_specs=(
            P(("dp", "expert"), None),
            P(),
            P(),
            P(),
            P(("dp", "expert"), None),
            P(),
            P("expert", None, None, "dp"),
            P("expert", None, "dp"),
            P("expert", "dp", None),
            P(),
        ),
        out_specs=P(("dp", "expert"), None),
        check_vma=False,
    )
```

```python
import jax
import jax.numpy as jnp
from jax import lax
from jax.sharding import PartitionSpec as P

TOPK = 4


EPS = 1e-05
LIMIT = 7.0
ALPHA = 1.702


def normalize(tokens, norm_gain):
    values = tokens.astype(jnp.float32)
    mean_square = jnp.mean(values * values, axis=-1, keepdims=True)
    return (values * lax.rsqrt(mean_square + EPS) * norm_gain).astype(jnp.bfloat16)


def routing(normed, router_weight, router_bias, expert_ids):
    logits = jnp.dot(normed, router_weight, preferred_element_type=jnp.float32) + router_bias
    expert_range = jnp.arange(logits.shape[1], dtype=jnp.int32)
    matches = expert_ids[:, :, None] == expert_range[None, None, :]
    picked = jnp.sum(jnp.where(matches, logits[:, None, :], 0.0), axis=2)
    powers = jnp.exp(picked)
    return powers / jnp.sum(powers, axis=1, keepdims=True)


def lookup(expert_ids, placement):
    expert_range = jnp.arange(placement.shape[0], dtype=jnp.int32)
    matches = expert_ids[:, :, None] == expert_range[None, None, :]
    return jnp.sum(jnp.where(matches, placement[None, None, :], 0), axis=2)


def slot_positions(columns, experts):
    flat_ids = columns.reshape(-1)
    expert_range = jnp.arange(experts, dtype=jnp.int32)
    onehot = (flat_ids[:, None] == expert_range[None, :]).astype(jnp.int32)
    before = jnp.cumsum(onehot, axis=0) - onehot
    return jnp.sum(before * onehot, axis=1).reshape(columns.shape)


def swiglu(gate_value, up_value):
    gate_value = jnp.minimum(gate_value, LIMIT)
    up_value = jnp.clip(up_value, -LIMIT, LIMIT)
    return (up_value + 1.0) * gate_value * jax.nn.sigmoid(ALPHA * gate_value)


def body(
    tokens,
    norm_gain,
    router_weight,
    router_bias,
    expert_ids,
    placement,
    gate_up,
    gate_up_bias,
    down_proj,
    down_bias,
):
    tok_dev = tokens.shape[0]
    model_width = tokens.shape[1]
    experts = placement.shape[0]
    capacity = max(2, 2 * tok_dev * TOPK // experts)
    expert_count = lax.axis_size("expert")
    normed = normalize(tokens, norm_gain)
    weights = routing(normed, router_weight, router_bias, expert_ids)
    columns = lookup(expert_ids, placement)
    target_row = columns * capacity + slot_positions(columns, experts)
    targets = jnp.arange(experts * capacity, dtype=jnp.int32)
    dispatch = jnp.sum(
        (target_row[:, :, None] == targets[None, None, :]).astype(jnp.int32), axis=1
    ).astype(jnp.bfloat16)
    outgoing = jnp.dot(dispatch.T, normed, preferred_element_type=jnp.float32).astype(jnp.bfloat16)
    outgoing = outgoing.reshape(experts, capacity, model_width)
    gate_weight = gate_up[0, 0]
    up_weight = gate_up[0, 1]
    gate_bias = gate_up_bias[0, 0]
    up_bias = gate_up_bias[0, 1]
    down_weight = down_proj[0]
    group_width = gate_weight.shape[1]
    chunks = 2 if capacity % 2 == 0 else 1
    width = capacity // chunks

    def expert_chunk(sent):
        row_block = lax.all_to_all(sent, "expert", split_axis=0, concat_axis=0, tiled=True)
        row_block = row_block.reshape(experts * width, model_width)
        flat_rows = lax.all_gather(row_block, "dp", axis=0, tiled=True)
        gate_value = jnp.dot(flat_rows, gate_weight, preferred_element_type=jnp.float32) + gate_bias
        up_value = jnp.dot(flat_rows, up_weight, preferred_element_type=jnp.float32) + up_bias
        hidden = swiglu(gate_value, up_value).astype(jnp.bfloat16)
        partials = jnp.dot(hidden, down_weight, preferred_element_type=jnp.float32).astype(
            jnp.bfloat16
        )
        reduced_parts = lax.psum_scatter(partials, "dp", scatter_dimension=0, tiled=True)
        reduced_parts = reduced_parts.reshape(expert_count, width, model_width)
        return lax.all_to_all(reduced_parts, "expert", split_axis=0, concat_axis=0, tiled=True)

    reduced = jnp.concatenate(
        [expert_chunk(outgoing[:, c * width : (c + 1) * width]) for c in range(chunks)], axis=1
    )
    reduced = reduced.astype(jnp.float32)
    reduced = reduced.reshape(experts, capacity, model_width) + down_bias[:, None, :]
    returned = reduced.astype(jnp.bfloat16).reshape(experts * capacity, model_width)
    picked = (
        returned[target_row.reshape(-1)].reshape(tok_dev, TOPK, model_width).astype(jnp.float32)
    )
    return jnp.sum(weights[:, :, None] * picked, axis=1).astype(jnp.bfloat16)


def solution(mesh):
    return jax.shard_map(
        body,
        mesh=mesh,
        in_specs=(
            P(("dp", "expert"), None),
            P(),
            P(),
            P(),
            P(("dp", "expert"), None),
            P(),
            P("expert", None, None, "dp"),
            P("expert", None, "dp"),
            P("expert", "dp", None),
            P(),
        ),
        out_specs=P(("dp", "expert"), None),
        check_vma=False,
    )
```

```python
import jax
import jax.numpy as jnp
from jax import lax
from jax.sharding import PartitionSpec as P
from jax.experimental.layout import Layout, with_layout_constraint

TOPK = 4


EPS = 1e-05
LIMIT = 7.0
ALPHA = 1.702


def normalize(tokens, norm_gain):
    values = tokens.astype(jnp.float32)
    mean_square = jnp.mean(values * values, axis=-1, keepdims=True)
    return (values * lax.rsqrt(mean_square + EPS) * norm_gain).astype(jnp.bfloat16)


def routing(normed, router_weight, router_bias, expert_ids):
    logits = jnp.dot(normed, router_weight, preferred_element_type=jnp.float32) + router_bias
    expert_range = jnp.arange(logits.shape[1], dtype=jnp.int32)
    matches = expert_ids[:, :, None] == expert_range[None, None, :]
    picked = jnp.sum(jnp.where(matches, logits[:, None, :], 0.0), axis=2)
    powers = jnp.exp(picked)
    return powers / jnp.sum(powers, axis=1, keepdims=True)


def lookup(expert_ids, placement):
    expert_range = jnp.arange(placement.shape[0], dtype=jnp.int32)
    matches = expert_ids[:, :, None] == expert_range[None, None, :]
    return jnp.sum(jnp.where(matches, placement[None, None, :], 0), axis=2)


def slot_positions(columns, experts):
    flat_ids = columns.reshape(-1)
    expert_range = jnp.arange(experts, dtype=jnp.int32)
    onehot = (flat_ids[:, None] == expert_range[None, :]).astype(jnp.int32)
    before = jnp.cumsum(onehot, axis=0) - onehot
    return jnp.sum(before * onehot, axis=1).reshape(columns.shape)


def swiglu(gate_value, up_value):
    gate_value = jnp.minimum(gate_value, LIMIT)
    up_value = jnp.clip(up_value, -LIMIT, LIMIT)
    return (up_value + 1.0) * gate_value * jax.nn.sigmoid(ALPHA * gate_value)


def body(
    tokens,
    norm_gain,
    router_weight,
    router_bias,
    expert_ids,
    placement,
    gate_up,
    gate_up_bias,
    down_proj,
    down_bias,
):
    tok_dev = tokens.shape[0]
    model_width = tokens.shape[1]
    experts = placement.shape[0]
    capacity = max(2, 2 * tok_dev * TOPK // experts)
    expert_count = lax.axis_size("expert")
    normed = normalize(tokens, norm_gain)
    weights = routing(normed, router_weight, router_bias, expert_ids)
    columns = lookup(expert_ids, placement)
    target_row = columns * capacity + slot_positions(columns, experts)
    targets = jnp.arange(experts * capacity, dtype=jnp.int32)
    dispatch = jnp.sum(
        (target_row[:, :, None] == targets[None, None, :]).astype(jnp.int32), axis=1
    ).astype(jnp.bfloat16)
    outgoing = jnp.dot(dispatch.T, normed, preferred_element_type=jnp.float32).astype(jnp.bfloat16)
    outgoing = with_layout_constraint(outgoing, Layout(major_to_minor=(0, 1)))
    outgoing = outgoing.reshape(experts, capacity, model_width)
    gate_weight = gate_up[0, 0]
    up_weight = gate_up[0, 1]
    gate_bias = gate_up_bias[0, 0]
    up_bias = gate_up_bias[0, 1]
    down_weight = down_proj[0]
    group_width = gate_weight.shape[1]
    row_block = lax.all_to_all(outgoing, "expert", split_axis=0, concat_axis=0, tiled=True)
    row_block = row_block.reshape(experts * capacity, model_width)
    flat_rows = lax.all_gather(row_block, "dp", axis=0, tiled=True)
    gate_value = jnp.dot(flat_rows, gate_weight, preferred_element_type=jnp.float32) + gate_bias
    up_value = jnp.dot(flat_rows, up_weight, preferred_element_type=jnp.float32) + up_bias
    hidden = swiglu(gate_value, up_value).astype(jnp.bfloat16)
    partials = jnp.dot(hidden, down_weight, preferred_element_type=jnp.float32).astype(jnp.bfloat16)
    partials = with_layout_constraint(partials, Layout(major_to_minor=(0, 1)))
    reduced_parts = lax.psum_scatter(partials, "dp", scatter_dimension=0, tiled=True)
    reduced_parts = reduced_parts.reshape(expert_count, capacity, model_width)
    reduced = lax.all_to_all(reduced_parts, "expert", split_axis=0, concat_axis=0, tiled=True)
    reduced = reduced.astype(jnp.float32)
    reduced = reduced.reshape(experts, capacity, model_width) + down_bias[:, None, :]
    returned = reduced.astype(jnp.bfloat16).reshape(experts * capacity, model_width)
    picked = (
        returned[target_row.reshape(-1)].reshape(tok_dev, TOPK, model_width).astype(jnp.float32)
    )
    return jnp.sum(weights[:, :, None] * picked, axis=1).astype(jnp.bfloat16)


def solution(mesh):
    return jax.shard_map(
        body,
        mesh=mesh,
        in_specs=(
            P(("dp", "expert"), None),
            P(),
            P(),
            P(),
            P(("dp", "expert"), None),
            P(),
            P("expert", None, None, "dp"),
            P("expert", None, "dp"),
            P("expert", "dp", None),
            P(),
        ),
        out_specs=P(("dp", "expert"), None),
        check_vma=False,
    )
```

```python
import jax
import jax.numpy as jnp
from jax import lax
from jax.sharding import PartitionSpec as P
from jax.experimental.layout import Layout, with_layout_constraint

TOPK = 4


EPS = 1e-05
LIMIT = 7.0
ALPHA = 1.702


def normalize(tokens, norm_gain):
    values = tokens.astype(jnp.float32)
    mean_square = jnp.mean(values * values, axis=-1, keepdims=True)
    return (values * lax.rsqrt(mean_square + EPS) * norm_gain).astype(jnp.bfloat16)


def routing(normed, router_weight, router_bias, expert_ids):
    logits = jnp.dot(normed, router_weight, preferred_element_type=jnp.float32) + router_bias
    expert_range = jnp.arange(logits.shape[1], dtype=jnp.int32)
    matches = expert_ids[:, :, None] == expert_range[None, None, :]
    picked = jnp.sum(jnp.where(matches, logits[:, None, :], 0.0), axis=2)
    powers = jnp.exp(picked)
    return powers / jnp.sum(powers, axis=1, keepdims=True)


def lookup(expert_ids, placement):
    expert_range = jnp.arange(placement.shape[0], dtype=jnp.int32)
    matches = expert_ids[:, :, None] == expert_range[None, None, :]
    return jnp.sum(jnp.where(matches, placement[None, None, :], 0), axis=2)


def slot_positions(columns, experts):
    flat_ids = columns.reshape(-1)
    expert_range = jnp.arange(experts, dtype=jnp.int32)
    onehot = (flat_ids[:, None] == expert_range[None, :]).astype(jnp.int32)
    before = jnp.cumsum(onehot, axis=0) - onehot
    return jnp.sum(before * onehot, axis=1).reshape(columns.shape)


def swiglu(gate_value, up_value):
    gate_value = jnp.minimum(gate_value, LIMIT)
    up_value = jnp.clip(up_value, -LIMIT, LIMIT)
    return (up_value + 1.0) * gate_value * jax.nn.sigmoid(ALPHA * gate_value)


def body(
    tokens,
    norm_gain,
    router_weight,
    router_bias,
    expert_ids,
    placement,
    gate_up,
    gate_up_bias,
    down_proj,
    down_bias,
):
    tok_dev = tokens.shape[0]
    model_width = tokens.shape[1]
    experts = placement.shape[0]
    capacity = max(2, 2 * tok_dev * TOPK // experts)
    expert_count = lax.axis_size("expert")
    dp_count = lax.axis_size("dp")
    normed = normalize(tokens, norm_gain)
    weights = routing(normed, router_weight, router_bias, expert_ids)
    columns = lookup(expert_ids, placement)
    target_row = columns * capacity + slot_positions(columns, experts)
    targets = jnp.arange(experts * capacity, dtype=jnp.int32)
    dispatch = jnp.sum(
        (target_row[:, :, None] == targets[None, None, :]).astype(jnp.int32), axis=1
    ).astype(jnp.bfloat16)
    outgoing = jnp.dot(dispatch.T, normed, preferred_element_type=jnp.float32).astype(jnp.bfloat16)
    outgoing = with_layout_constraint(outgoing, Layout(major_to_minor=(0, 1)))
    outgoing = outgoing.reshape(experts, capacity, model_width)
    gate_weight = gate_up[0, 0]
    up_weight = gate_up[0, 1]
    gate_bias = gate_up_bias[0, 0]
    up_bias = gate_up_bias[0, 1]
    down_weight = down_proj[0]
    group_width = gate_weight.shape[1]
    row_block = lax.all_to_all(outgoing, "expert", split_axis=0, concat_axis=0, tiled=True)
    row_block = row_block.reshape(experts * capacity, model_width)
    flat_rows = lax.all_gather(row_block, "dp", axis=0, tiled=True)
    gate_value = jnp.dot(flat_rows, gate_weight, preferred_element_type=jnp.float32) + gate_bias
    up_value = jnp.dot(flat_rows, up_weight, preferred_element_type=jnp.float32) + up_bias
    hidden = swiglu(gate_value, up_value).astype(jnp.bfloat16)
    hidden = hidden.reshape(dp_count, -1, hidden.shape[-1])
    partials = jnp.einsum("grf,fo->gro", hidden, down_weight, preferred_element_type=jnp.float32)
    partials = partials.astype(jnp.bfloat16)
    partials = with_layout_constraint(partials, Layout(major_to_minor=(0, 1, 2)))
    partials = partials.reshape(-1, model_width)
    reduced_parts = lax.psum_scatter(partials, "dp", scatter_dimension=0, tiled=True)
    reduced_parts = reduced_parts.reshape(expert_count, capacity, model_width)
    reduced = lax.all_to_all(reduced_parts, "expert", split_axis=0, concat_axis=0, tiled=True)
    reduced = reduced.astype(jnp.float32)
    reduced = reduced.reshape(experts, capacity, model_width) + down_bias[:, None, :]
    returned = reduced.astype(jnp.bfloat16).reshape(experts * capacity, model_width)
    picked = (
        returned[target_row.reshape(-1)].reshape(tok_dev, TOPK, model_width).astype(jnp.float32)
    )
    return jnp.sum(weights[:, :, None] * picked, axis=1).astype(jnp.bfloat16)


def solution(mesh):
    return jax.shard_map(
        body,
        mesh=mesh,
        in_specs=(
            P(("dp", "expert"), None),
            P(),
            P(),
            P(),
            P(("dp", "expert"), None),
            P(),
            P("expert", None, None, "dp"),
            P("expert", None, "dp"),
            P("expert", "dp", None),
            P(),
        ),
        out_specs=P(("dp", "expert"), None),
        check_vma=False,
    )
```

```python
import jax
import jax.numpy as jnp
from jax import lax
from jax.sharding import PartitionSpec as P
from jax.experimental.layout import Layout, with_layout_constraint

TOPK = 4


EPS = 1e-05
LIMIT = 7.0
ALPHA = 1.702


def normalize(tokens, norm_gain):
    values = tokens.astype(jnp.float32)
    mean_square = jnp.mean(values * values, axis=-1, keepdims=True)
    return (values * lax.rsqrt(mean_square + EPS) * norm_gain).astype(jnp.bfloat16)


def routing(normed, router_weight, router_bias, expert_ids):
    logits = jnp.dot(normed, router_weight, preferred_element_type=jnp.float32) + router_bias
    expert_range = jnp.arange(logits.shape[1], dtype=jnp.int32)
    matches = expert_ids[:, :, None] == expert_range[None, None, :]
    picked = jnp.sum(jnp.where(matches, logits[:, None, :], 0.0), axis=2)
    powers = jnp.exp(picked)
    return powers / jnp.sum(powers, axis=1, keepdims=True)


def lookup(expert_ids, placement):
    expert_range = jnp.arange(placement.shape[0], dtype=jnp.int32)
    matches = expert_ids[:, :, None] == expert_range[None, None, :]
    return jnp.sum(jnp.where(matches, placement[None, None, :], 0), axis=2)


def slot_positions(columns, experts):
    flat_ids = columns.reshape(-1)
    expert_range = jnp.arange(experts, dtype=jnp.int32)
    onehot = (flat_ids[:, None] == expert_range[None, :]).astype(jnp.int32)
    before = jnp.cumsum(onehot, axis=0) - onehot
    return jnp.sum(before * onehot, axis=1).reshape(columns.shape)


def swiglu(gate_value, up_value):
    gate_value = jnp.minimum(gate_value, LIMIT)
    up_value = jnp.clip(up_value, -LIMIT, LIMIT)
    return (up_value + 1.0) * gate_value * jax.nn.sigmoid(ALPHA * gate_value)


def body(
    tokens,
    norm_gain,
    router_weight,
    router_bias,
    expert_ids,
    placement,
    gate_up,
    gate_up_bias,
    down_proj,
    down_bias,
):
    tok_dev = tokens.shape[0]
    model_width = tokens.shape[1]
    experts = placement.shape[0]
    capacity = max(2, 2 * tok_dev * TOPK // experts)
    expert_count = lax.axis_size("expert")
    dp_count = lax.axis_size("dp")
    normed = normalize(tokens, norm_gain)
    weights = routing(normed, router_weight, router_bias, expert_ids)
    columns = lookup(expert_ids, placement)
    slots = slot_positions(columns, experts)
    target_row = columns * capacity + slots
    targets = jnp.arange(experts * capacity, dtype=jnp.int32)
    dispatch = jnp.sum(
        (target_row[:, :, None] == targets[None, None, :]).astype(jnp.int32), axis=1
    ).astype(jnp.bfloat16)
    outgoing = jnp.dot(dispatch.T, normed, preferred_element_type=jnp.float32).astype(jnp.bfloat16)
    outgoing = with_layout_constraint(outgoing, Layout(major_to_minor=(0, 1)))
    outgoing = outgoing.reshape(experts, capacity, model_width)
    gate_weight = gate_up[0, 0]
    up_weight = gate_up[0, 1]
    gate_bias = gate_up_bias[0, 0]
    up_bias = gate_up_bias[0, 1]
    down_weight = down_proj[0]
    group_width = gate_weight.shape[1]
    row_block = lax.all_to_all(outgoing, "expert", split_axis=0, concat_axis=0, tiled=True)
    row_block = row_block.reshape(experts * capacity, model_width)
    flat_rows = lax.all_gather(row_block, "dp", axis=0, tiled=True)
    gate_value = jnp.dot(flat_rows, gate_weight, preferred_element_type=jnp.float32) + gate_bias
    up_value = jnp.dot(flat_rows, up_weight, preferred_element_type=jnp.float32) + up_bias
    hidden = swiglu(gate_value, up_value).astype(jnp.bfloat16)
    hidden = hidden.reshape(dp_count, -1, hidden.shape[-1])
    partials = jnp.einsum("grf,fo->gro", hidden, down_weight, preferred_element_type=jnp.float32)
    partials = partials.astype(jnp.bfloat16)
    partials = with_layout_constraint(partials, Layout(major_to_minor=(0, 1, 2)))
    partials = partials.reshape(-1, model_width)
    reduced_parts = lax.psum_scatter(partials, "dp", scatter_dimension=0, tiled=True)
    reduced_parts = reduced_parts.reshape(expert_count, capacity, model_width)
    reduced = lax.all_to_all(reduced_parts, "expert", split_axis=0, concat_axis=0, tiled=True)
    reduced = reduced.astype(jnp.float32)
    reduced = reduced.reshape(experts, capacity, model_width) + down_bias[:, None, :]
    returned = reduced.astype(jnp.bfloat16)
    picked = (
        returned[columns, slots].astype(jnp.float32)
    )
    return jnp.sum(weights[:, :, None] * picked, axis=1).astype(jnp.bfloat16)


def solution(mesh):
    return jax.shard_map(
        body,
        mesh=mesh,
        in_specs=(
            P(("dp", "expert"), None),
            P(),
            P(),
            P(),
            P(("dp", "expert"), None),
            P(),
            P("expert", None, None, "dp"),
            P("expert", None, "dp"),
            P("expert", "dp", None),
            P(),
        ),
        out_specs=P(("dp", "expert"), None),
        check_vma=False,
    )
```

```python
import jax
import jax.numpy as jnp
from jax import lax
from jax.sharding import PartitionSpec as P
from jax.experimental.layout import Layout, with_layout_constraint

TOPK = 4


EPS = 1e-05
LIMIT = 7.0
ALPHA = 1.702


def normalize(tokens, norm_gain):
    values = tokens.astype(jnp.float32)
    mean_square = jnp.mean(values * values, axis=-1, keepdims=True)
    return (values * lax.rsqrt(mean_square + EPS) * norm_gain).astype(jnp.bfloat16)


def routing(normed, router_weight, router_bias, expert_ids):
    logits = jnp.dot(normed, router_weight, preferred_element_type=jnp.float32) + router_bias
    expert_range = jnp.arange(logits.shape[1], dtype=jnp.int32)
    matches = expert_ids[:, :, None] == expert_range[None, None, :]
    picked = jnp.sum(jnp.where(matches, logits[:, None, :], 0.0), axis=2)
    powers = jnp.exp(picked)
    return powers / jnp.sum(powers, axis=1, keepdims=True)


def lookup(expert_ids, placement):
    expert_range = jnp.arange(placement.shape[0], dtype=jnp.int32)
    matches = expert_ids[:, :, None] == expert_range[None, None, :]
    return jnp.sum(jnp.where(matches, placement[None, None, :], 0), axis=2)


def slot_positions(columns, experts):
    flat_ids = columns.reshape(-1)
    expert_range = jnp.arange(experts, dtype=jnp.int32)
    onehot = (flat_ids[:, None] == expert_range[None, :]).astype(jnp.int32)
    before = jnp.cumsum(onehot, axis=0) - onehot
    return jnp.sum(before * onehot, axis=1).reshape(columns.shape)


def swiglu(gate_value, up_value):
    gate_value = jnp.minimum(gate_value, LIMIT)
    up_value = jnp.clip(up_value, -LIMIT, LIMIT)
    return (up_value + 1.0) * gate_value * jax.nn.sigmoid(ALPHA * gate_value)


def body(
    tokens,
    norm_gain,
    router_weight,
    router_bias,
    expert_ids,
    placement,
    gate_up,
    gate_up_bias,
    down_proj,
    down_bias,
):
    tok_dev = tokens.shape[0]
    model_width = tokens.shape[1]
    experts = placement.shape[0]
    capacity = max(2, 2 * tok_dev * TOPK // experts)
    expert_count = lax.axis_size("expert")
    dp_count = lax.axis_size("dp")
    normed = normalize(tokens, norm_gain)
    weights = routing(normed, router_weight, router_bias, expert_ids)
    columns = lookup(expert_ids, placement)
    slots = slot_positions(columns, experts)
    target_row = columns * capacity + slots
    targets = jnp.arange(experts * capacity, dtype=jnp.int32)
    dispatch = jnp.sum(
        (target_row[:, :, None] == targets[None, None, :]).astype(jnp.int32), axis=1
    ).astype(jnp.bfloat16)
    outgoing = jnp.dot(dispatch.T, normed, preferred_element_type=jnp.float32).astype(jnp.bfloat16)
    outgoing = with_layout_constraint(outgoing, Layout(major_to_minor=(0, 1)))
    outgoing = outgoing.reshape(experts, capacity, model_width)
    gate_weight = gate_up[0, 0]
    up_weight = gate_up[0, 1]
    gate_bias = gate_up_bias[0, 0]
    up_bias = gate_up_bias[0, 1]
    down_weight = down_proj[0]
    group_width = gate_weight.shape[1]
    row_block = lax.all_to_all(outgoing, "expert", split_axis=0, concat_axis=0, tiled=True)
    row_block = row_block.reshape(experts * capacity, model_width)
    flat_rows = lax.all_gather(row_block, "dp", axis=0, tiled=True)
    gate_value = jnp.dot(flat_rows, gate_weight, preferred_element_type=jnp.float32) + gate_bias
    up_value = jnp.dot(flat_rows, up_weight, preferred_element_type=jnp.float32) + up_bias
    hidden = swiglu(gate_value, up_value).astype(jnp.bfloat16)
    hidden = hidden.reshape(dp_count, -1, hidden.shape[-1])
    partials = jnp.einsum("grf,fo->gro", hidden, down_weight, preferred_element_type=jnp.float32)
    partials = partials.astype(jnp.bfloat16)
    partials = with_layout_constraint(partials, Layout(major_to_minor=(0, 1, 2)))
    partials = partials.reshape(-1, model_width)
    reduced_parts = lax.psum_scatter(partials, "dp", scatter_dimension=0, tiled=True)
    reduced_parts = reduced_parts.reshape(expert_count, capacity, model_width)
    reduced = lax.all_to_all(reduced_parts, "expert", split_axis=0, concat_axis=0, tiled=True)
    reduced = reduced.reshape(experts, capacity, model_width)
    mixed = jnp.zeros((tok_dev, model_width), jnp.float32)
    for k in range(TOPK):
        row = reduced[columns[:, k], slots[:, k]].astype(jnp.float32) + down_bias[columns[:, k]]
        row = row.astype(jnp.bfloat16).astype(jnp.float32)
        mixed = mixed + weights[:, k : k + 1] * row
    return mixed.astype(jnp.bfloat16)


def solution(mesh):
    return jax.shard_map(
        body,
        mesh=mesh,
        in_specs=(
            P(("dp", "expert"), None),
            P(),
            P(),
            P(),
            P(("dp", "expert"), None),
            P(),
            P("expert", None, None, "dp"),
            P("expert", None, "dp"),
            P("expert", "dp", None),
            P(),
        ),
        out_specs=P(("dp", "expert"), None),
        check_vma=False,
    )
```

```python
import jax
import jax.numpy as jnp
from jax import lax
from jax.sharding import PartitionSpec as P
from jax.experimental.layout import Layout, with_layout_constraint

TOPK = 4


EPS = 1e-05
LIMIT = 7.0
ALPHA = 1.702


def normalize(tokens, norm_gain):
    values = tokens.astype(jnp.float32)
    mean_square = jnp.mean(values * values, axis=-1, keepdims=True)
    return (values * lax.rsqrt(mean_square + EPS) * norm_gain).astype(jnp.bfloat16)


def routing(normed, router_weight, router_bias, expert_ids):
    logits = jnp.dot(normed, router_weight, preferred_element_type=jnp.float32) + router_bias
    expert_range = jnp.arange(logits.shape[1], dtype=jnp.int32)
    matches = expert_ids[:, :, None] == expert_range[None, None, :]
    picked = jnp.sum(jnp.where(matches, logits[:, None, :], 0.0), axis=2)
    powers = jnp.exp(picked)
    return powers / jnp.sum(powers, axis=1, keepdims=True)


def lookup(expert_ids, placement):
    expert_range = jnp.arange(placement.shape[0], dtype=jnp.int32)
    matches = expert_ids[:, :, None] == expert_range[None, None, :]
    return jnp.sum(jnp.where(matches, placement[None, None, :], 0), axis=2)


def slot_positions(columns, experts):
    flat_ids = columns.reshape(-1)
    order = jnp.arange(flat_ids.shape[0], dtype=jnp.int32)
    earlier = (flat_ids[:, None] == flat_ids[None, :]) & (order[None, :] < order[:, None])
    return jnp.sum(earlier.astype(jnp.int32), axis=1).reshape(columns.shape)


def swiglu(gate_value, up_value):
    gate_value = jnp.minimum(gate_value, LIMIT)
    up_value = jnp.clip(up_value, -LIMIT, LIMIT)
    return (up_value + 1.0) * gate_value * jax.nn.sigmoid(ALPHA * gate_value)


def body(
    tokens,
    norm_gain,
    router_weight,
    router_bias,
    expert_ids,
    placement,
    gate_up,
    gate_up_bias,
    down_proj,
    down_bias,
):
    tok_dev = tokens.shape[0]
    model_width = tokens.shape[1]
    experts = placement.shape[0]
    capacity = max(2, 2 * tok_dev * TOPK // experts)
    expert_count = lax.axis_size("expert")
    dp_count = lax.axis_size("dp")
    normed = normalize(tokens, norm_gain)
    weights = routing(normed, router_weight, router_bias, expert_ids)
    columns = lookup(expert_ids, placement)
    slots = slot_positions(columns, experts)
    target_row = columns * capacity + slots
    targets = jnp.arange(experts * capacity, dtype=jnp.int32)
    dispatch = jnp.sum(
        (target_row[:, :, None] == targets[None, None, :]).astype(jnp.int32), axis=1
    ).astype(jnp.bfloat16)
    outgoing = jnp.dot(dispatch.T, normed, preferred_element_type=jnp.float32).astype(jnp.bfloat16)
    outgoing = with_layout_constraint(outgoing, Layout(major_to_minor=(0, 1)))
    outgoing = outgoing.reshape(experts, capacity, model_width)
    gate_weight = gate_up[0, 0]
    up_weight = gate_up[0, 1]
    gate_bias = gate_up_bias[0, 0]
    up_bias = gate_up_bias[0, 1]
    down_weight = down_proj[0]
    group_width = gate_weight.shape[1]
    row_block = lax.all_to_all(outgoing, "expert", split_axis=0, concat_axis=0, tiled=True)
    row_block = row_block.reshape(experts * capacity, model_width)
    flat_rows = lax.all_gather(row_block, "dp", axis=0, tiled=True)
    gate_value = jnp.dot(flat_rows, gate_weight, preferred_element_type=jnp.float32) + gate_bias
    up_value = jnp.dot(flat_rows, up_weight, preferred_element_type=jnp.float32) + up_bias
    hidden = swiglu(gate_value, up_value).astype(jnp.bfloat16)
    hidden = hidden.reshape(dp_count, -1, hidden.shape[-1])
    partials = jnp.einsum("grf,fo->gro", hidden, down_weight, preferred_element_type=jnp.float32)
    partials = partials.astype(jnp.bfloat16)
    partials = with_layout_constraint(partials, Layout(major_to_minor=(0, 1, 2)))
    partials = partials.reshape(-1, model_width)
    reduced_parts = lax.psum_scatter(partials, "dp", scatter_dimension=0, tiled=True)
    reduced_parts = reduced_parts.reshape(expert_count, capacity, model_width)
    reduced = lax.all_to_all(reduced_parts, "expert", split_axis=0, concat_axis=0, tiled=True)
    reduced = reduced.astype(jnp.float32)
    reduced = reduced.reshape(experts, capacity, model_width) + down_bias[:, None, :]
    returned = reduced.astype(jnp.bfloat16)
    picked = (
        returned[columns, slots].astype(jnp.float32)
    )
    return jnp.sum(weights[:, :, None] * picked, axis=1).astype(jnp.bfloat16)


def solution(mesh):
    return jax.shard_map(
        body,
        mesh=mesh,
        in_specs=(
            P(("dp", "expert"), None),
            P(),
            P(),
            P(),
            P(("dp", "expert"), None),
            P(),
            P("expert", None, None, "dp"),
            P("expert", None, "dp"),
            P("expert", "dp", None),
            P(),
        ),
        out_specs=P(("dp", "expert"), None),
        check_vma=False,
    )
```

```python
import jax
import jax.numpy as jnp
from jax import lax
from jax.sharding import PartitionSpec as P
from jax.experimental.layout import Layout, with_layout_constraint

TOPK = 4


EPS = 1e-05
LIMIT = 7.0
ALPHA = 1.702


def normalize(tokens, norm_gain):
    values = tokens.astype(jnp.float32)
    mean_square = jnp.mean(values * values, axis=-1, keepdims=True)
    return (values * lax.rsqrt(mean_square + EPS) * norm_gain).astype(jnp.bfloat16)


def routing(normed, router_weight, router_bias, expert_ids):
    logits = jnp.dot(normed, router_weight, preferred_element_type=jnp.float32) + router_bias
    expert_range = jnp.arange(logits.shape[1], dtype=jnp.int32)
    matches = expert_ids[:, :, None] == expert_range[None, None, :]
    picked = jnp.sum(jnp.where(matches, logits[:, None, :], 0.0), axis=2)
    powers = jnp.exp(picked)
    return powers / jnp.sum(powers, axis=1, keepdims=True)


def lookup(expert_ids, placement):
    return jnp.take(placement, expert_ids, mode="clip")


def slot_positions(columns, experts):
    flat_ids = columns.reshape(-1)
    order = jnp.arange(flat_ids.shape[0], dtype=jnp.int32)
    earlier = (flat_ids[:, None] == flat_ids[None, :]) & (order[None, :] < order[:, None])
    return jnp.sum(earlier.astype(jnp.int32), axis=1).reshape(columns.shape)


def swiglu(gate_value, up_value):
    gate_value = jnp.minimum(gate_value, LIMIT)
    up_value = jnp.clip(up_value, -LIMIT, LIMIT)
    return (up_value + 1.0) * gate_value * jax.nn.sigmoid(ALPHA * gate_value)


def body(
    tokens,
    norm_gain,
    router_weight,
    router_bias,
    expert_ids,
    placement,
    gate_up,
    gate_up_bias,
    down_proj,
    down_bias,
):
    tok_dev = tokens.shape[0]
    model_width = tokens.shape[1]
    experts = placement.shape[0]
    capacity = max(2, 2 * tok_dev * TOPK // experts)
    expert_count = lax.axis_size("expert")
    dp_count = lax.axis_size("dp")
    normed = normalize(tokens, norm_gain)
    weights = routing(normed, router_weight, router_bias, expert_ids)
    columns = lookup(expert_ids, placement)
    slots = slot_positions(columns, experts)
    target_row = columns * capacity + slots
    targets = jnp.arange(experts * capacity, dtype=jnp.int32)
    dispatch = jnp.sum(
        (target_row[:, :, None] == targets[None, None, :]).astype(jnp.int32), axis=1
    ).astype(jnp.bfloat16)
    outgoing = jnp.dot(dispatch.T, normed, preferred_element_type=jnp.float32).astype(jnp.bfloat16)
    outgoing = with_layout_constraint(outgoing, Layout(major_to_minor=(0, 1)))
    outgoing = outgoing.reshape(experts, capacity, model_width)
    gate_weight = gate_up[0, 0]
    up_weight = gate_up[0, 1]
    gate_bias = gate_up_bias[0, 0]
    up_bias = gate_up_bias[0, 1]
    down_weight = down_proj[0]
    group_width = gate_weight.shape[1]
    row_block = lax.all_to_all(outgoing, "expert", split_axis=0, concat_axis=0, tiled=True)
    row_block = row_block.reshape(experts * capacity, model_width)
    flat_rows = lax.all_gather(row_block, "dp", axis=0, tiled=True)
    gate_value = jnp.dot(flat_rows, gate_weight, preferred_element_type=jnp.float32) + gate_bias
    up_value = jnp.dot(flat_rows, up_weight, preferred_element_type=jnp.float32) + up_bias
    hidden = swiglu(gate_value, up_value).astype(jnp.bfloat16)
    hidden = hidden.reshape(dp_count, -1, hidden.shape[-1])
    partials = jnp.einsum("grf,fo->gro", hidden, down_weight, preferred_element_type=jnp.float32)
    partials = partials.astype(jnp.bfloat16)
    partials = with_layout_constraint(partials, Layout(major_to_minor=(0, 1, 2)))
    partials = partials.reshape(-1, model_width)
    reduced_parts = lax.psum_scatter(partials, "dp", scatter_dimension=0, tiled=True)
    reduced_parts = reduced_parts.reshape(expert_count, capacity, model_width)
    reduced = lax.all_to_all(reduced_parts, "expert", split_axis=0, concat_axis=0, tiled=True)
    reduced = reduced.astype(jnp.float32)
    reduced = reduced.reshape(experts, capacity, model_width) + down_bias[:, None, :]
    returned = reduced.astype(jnp.bfloat16)
    picked = (
        returned[columns, slots].astype(jnp.float32)
    )
    return jnp.sum(weights[:, :, None] * picked, axis=1).astype(jnp.bfloat16)


def solution(mesh):
    return jax.shard_map(
        body,
        mesh=mesh,
        in_specs=(
            P(("dp", "expert"), None),
            P(),
            P(),
            P(),
            P(("dp", "expert"), None),
            P(),
            P("expert", None, None, "dp"),
            P("expert", None, "dp"),
            P("expert", "dp", None),
            P(),
        ),
        out_specs=P(("dp", "expert"), None),
        check_vma=False,
    )
```

```python
import jax
import jax.numpy as jnp
from jax import lax
from jax.sharding import PartitionSpec as P
from jax.experimental.layout import Layout, with_layout_constraint

TOPK = 4


EPS = 1e-05
LIMIT = 7.0
ALPHA = 1.702


def normalize(tokens, norm_gain):
    values = tokens.astype(jnp.float32)
    mean_square = jnp.mean(values * values, axis=-1, keepdims=True)
    return (values * lax.rsqrt(mean_square + EPS) * norm_gain).astype(jnp.bfloat16)


def routing(normed, router_weight, router_bias, expert_ids):
    logits = jnp.dot(normed, router_weight, preferred_element_type=jnp.float32) + router_bias
    expert_range = jnp.arange(logits.shape[1], dtype=jnp.int32)
    matches = expert_ids[:, :, None] == expert_range[None, None, :]
    picked = jnp.sum(jnp.where(matches, logits[:, None, :], 0.0), axis=2)
    powers = jnp.exp(picked)
    return powers / jnp.sum(powers, axis=1, keepdims=True)


def lookup(expert_ids, placement):
    return jnp.take(placement, expert_ids, mode="clip")


def slot_positions(columns, experts):
    flat_ids = columns.reshape(-1)
    order = jnp.arange(flat_ids.shape[0], dtype=jnp.int32)
    earlier = (flat_ids[:, None] == flat_ids[None, :]) & (order[None, :] < order[:, None])
    return jnp.sum(earlier.astype(jnp.int32), axis=1).reshape(columns.shape)


def swiglu(gate_value, up_value):
    gate_value = jnp.minimum(gate_value, LIMIT)
    up_value = jnp.clip(up_value, -LIMIT, LIMIT)
    return (up_value + 1.0) * gate_value * jax.nn.sigmoid(ALPHA * gate_value)


def body(
    tokens,
    norm_gain,
    router_weight,
    router_bias,
    expert_ids,
    placement,
    gate_up,
    gate_up_bias,
    down_proj,
    down_bias,
):
    tok_dev = tokens.shape[0]
    model_width = tokens.shape[1]
    experts = placement.shape[0]
    capacity = max(2, 2 * tok_dev * TOPK // experts)
    expert_count = lax.axis_size("expert")
    dp_count = lax.axis_size("dp")
    normed = normalize(tokens, norm_gain)
    weights = routing(normed, router_weight, router_bias, expert_ids)
    columns = lookup(expert_ids, placement)
    slots = slot_positions(columns, experts)
    target_row = columns * capacity + slots
    targets = jnp.arange(experts * capacity, dtype=jnp.int32)
    dispatch = jnp.sum(
        (target_row[:, :, None] == targets[None, None, :]).astype(jnp.int32), axis=1
    ).astype(jnp.bfloat16)
    outgoing = jnp.dot(dispatch.T, normed, preferred_element_type=jnp.float32).astype(jnp.bfloat16)
    outgoing = with_layout_constraint(outgoing, Layout(major_to_minor=(0, 1)))
    outgoing = outgoing.reshape(experts, capacity, model_width)
    gate_weight = gate_up[0, 0]
    up_weight = gate_up[0, 1]
    gate_bias = gate_up_bias[0, 0]
    up_bias = gate_up_bias[0, 1]
    down_weight = down_proj[0]
    group_width = gate_weight.shape[1]
    row_block = lax.all_to_all(outgoing, "expert", split_axis=0, concat_axis=0, tiled=True)
    row_block = row_block.reshape(experts * capacity, model_width)
    flat_rows = lax.all_gather(row_block, "dp", axis=0, tiled=True)
    gate_value = jnp.dot(flat_rows, gate_weight, preferred_element_type=jnp.float32) + gate_bias
    up_value = jnp.dot(flat_rows, up_weight, preferred_element_type=jnp.float32) + up_bias
    hidden = swiglu(gate_value, up_value).astype(jnp.bfloat16)
    hidden = hidden.reshape(dp_count, -1, hidden.shape[-1])
    partials = jnp.einsum("grf,fo->gro", hidden, down_weight, preferred_element_type=jnp.float32)
    partials = partials.astype(jnp.bfloat16)
    partials = with_layout_constraint(partials, Layout(major_to_minor=(0, 1, 2)))
    partials = partials.reshape(-1, model_width)
    reduced_parts = lax.psum_scatter(partials, "dp", scatter_dimension=0, tiled=True)
    reduced_parts = reduced_parts.reshape(expert_count, capacity, model_width)
    reduced = lax.all_to_all(reduced_parts, "expert", split_axis=0, concat_axis=0, tiled=True)
    reduced = reduced.reshape(experts, capacity, model_width)
    picked = reduced[columns.T, slots.T].astype(jnp.float32) + down_bias[columns.T]
    picked = picked.astype(jnp.bfloat16).astype(jnp.float32)
    return jnp.sum(weights.T[:, :, None] * picked, axis=0).astype(jnp.bfloat16)


def solution(mesh):
    return jax.shard_map(
        body,
        mesh=mesh,
        in_specs=(
            P(("dp", "expert"), None),
            P(),
            P(),
            P(),
            P(("dp", "expert"), None),
            P(),
            P("expert", None, None, "dp"),
            P("expert", None, "dp"),
            P("expert", "dp", None),
            P(),
        ),
        out_specs=P(("dp", "expert"), None),
        check_vma=False,
    )
```

```python
import jax
import jax.numpy as jnp
from jax import lax
from jax.sharding import PartitionSpec as P
from jax.experimental.layout import Layout, with_layout_constraint

TOPK = 4


EPS = 1e-05
LIMIT = 7.0
ALPHA = 1.702


def normalize(tokens, norm_gain):
    values = tokens.astype(jnp.float32)
    mean_square = jnp.mean(values * values, axis=-1, keepdims=True)
    return (values * lax.rsqrt(mean_square + EPS) * norm_gain).astype(jnp.bfloat16)


def routing(normed, router_weight, router_bias, expert_ids):
    logits = jnp.dot(normed, router_weight, preferred_element_type=jnp.float32) + router_bias
    expert_range = jnp.arange(logits.shape[1], dtype=jnp.int32)
    matches = expert_ids[:, :, None] == expert_range[None, None, :]
    picked = jnp.sum(jnp.where(matches, logits[:, None, :], 0.0), axis=2)
    powers = jnp.exp(picked)
    return powers / jnp.sum(powers, axis=1, keepdims=True)


def lookup(expert_ids, placement):
    return jnp.take(placement, expert_ids, mode="clip")


def slot_positions(columns, experts):
    flat_ids = columns.reshape(-1)
    order = jnp.arange(flat_ids.shape[0], dtype=jnp.int32)
    earlier = (flat_ids[:, None] == flat_ids[None, :]) & (order[None, :] < order[:, None])
    return jnp.sum(earlier.astype(jnp.int32), axis=1).reshape(columns.shape)


def swiglu(gate_value, up_value):
    gate_value = jnp.minimum(gate_value, LIMIT)
    up_value = jnp.clip(up_value, -LIMIT, LIMIT)
    return (up_value + 1.0) * gate_value * jax.nn.sigmoid(ALPHA * gate_value)


def body(
    tokens,
    norm_gain,
    router_weight,
    router_bias,
    expert_ids,
    placement,
    gate_up,
    gate_up_bias,
    down_proj,
    down_bias,
):
    tok_dev = tokens.shape[0]
    model_width = tokens.shape[1]
    experts = placement.shape[0]
    capacity = max(2, 2 * tok_dev * TOPK // experts)
    expert_count = lax.axis_size("expert")
    dp_count = lax.axis_size("dp")
    normed = normalize(tokens, norm_gain)
    weights = routing(normed, router_weight, router_bias, expert_ids)
    columns = lookup(expert_ids, placement)
    columns = columns.T
    slots = slot_positions(columns, experts)
    target_row = columns * capacity + slots
    targets = jnp.arange(experts * capacity, dtype=jnp.int32)
    dispatch = jnp.sum(
        (target_row[:, :, None] == targets[None, None, :]).astype(jnp.int32), axis=0
    ).astype(jnp.bfloat16)
    outgoing = jnp.dot(dispatch.T, normed, preferred_element_type=jnp.float32).astype(jnp.bfloat16)
    outgoing = with_layout_constraint(outgoing, Layout(major_to_minor=(0, 1)))
    outgoing = outgoing.reshape(experts, capacity, model_width)
    gate_weight = gate_up[0, 0]
    up_weight = gate_up[0, 1]
    gate_bias = gate_up_bias[0, 0]
    up_bias = gate_up_bias[0, 1]
    down_weight = down_proj[0]
    group_width = gate_weight.shape[1]
    row_block = lax.all_to_all(outgoing, "expert", split_axis=0, concat_axis=0, tiled=True)
    row_block = row_block.reshape(experts * capacity, model_width)
    flat_rows = lax.all_gather(row_block, "dp", axis=0, tiled=True)
    gate_value = jnp.dot(flat_rows, gate_weight, preferred_element_type=jnp.float32) + gate_bias
    up_value = jnp.dot(flat_rows, up_weight, preferred_element_type=jnp.float32) + up_bias
    hidden = swiglu(gate_value, up_value).astype(jnp.bfloat16)
    hidden = hidden.reshape(dp_count, -1, hidden.shape[-1])
    partials = jnp.einsum("grf,fo->gro", hidden, down_weight, preferred_element_type=jnp.float32)
    partials = partials.astype(jnp.bfloat16)
    partials = with_layout_constraint(partials, Layout(major_to_minor=(0, 1, 2)))
    partials = partials.reshape(-1, model_width)
    reduced_parts = lax.psum_scatter(partials, "dp", scatter_dimension=0, tiled=True)
    reduced_parts = reduced_parts.reshape(expert_count, capacity, model_width)
    reduced = lax.all_to_all(reduced_parts, "expert", split_axis=0, concat_axis=0, tiled=True)
    reduced = reduced.reshape(experts, capacity, model_width)
    picked = reduced[columns, slots].astype(jnp.float32) + down_bias[columns]
    picked = picked.astype(jnp.bfloat16).astype(jnp.float32)
    return jnp.sum(weights.T[:, :, None] * picked, axis=0).astype(jnp.bfloat16)


def solution(mesh):
    return jax.shard_map(
        body,
        mesh=mesh,
        in_specs=(
            P(("dp", "expert"), None),
            P(),
            P(),
            P(),
            P(("dp", "expert"), None),
            P(),
            P("expert", None, None, "dp"),
            P("expert", None, "dp"),
            P("expert", "dp", None),
            P(),
        ),
        out_specs=P(("dp", "expert"), None),
        check_vma=False,
    )
```
